512 devices in a mesh: row: 16 (over y, core), col: 32 (over x, z).
Axes of the slice: x: 4, y: 8, z: 8, core: 2. Of those that a mesh axis runs over, the one named last changes fastest.
Arguments:
- vectors: bfloat16 [16, 32, 128, 384], P('row', 'col'), may hold values from -6 to 6
- near_blocks: bfloat16 [16, 32, 9, 384, 384], P('row', 'col'), may hold values from -0.15625 to 0.15625
- near_source: int32 [16, 32, 9], P('row', 'col'), may hold values from 0 to 8, each once within a row
- near_count: int32 [16, 32], P('row', 'col'), may hold values from 1 to 9
- basis_col: bfloat16 [16, 32, 64, 384], P('row', 'col'), may hold values from -0.3125 to 0.3125
- transfer_col: bfloat16 [16, 32, 64, 64], P('row', 'col'), may hold values from -0.125 to 0.125
- leaf_couple: bfloat16 [16, 32, 3, 29, 64, 64], P('row', 'col'), may hold values from -0.078125 to 0.078125
- coupling: bfloat16 [16, 16, 64, 64], P('row'), may hold values from -0.21875 to 0.21875
- distant_region_list: int32 [16, 16], P('row'), may hold values from 0 to 15, each once within a row
- transfer_row: bfloat16 [16, 32, 64, 64], P('row', 'col'), may hold values from -0.75 to 0.75
- basis_row: bfloat16 [16, 32, 64, 384], P('row', 'col'), may hold values from -0.75 to 0.75
Outputs:
- product: bfloat16 [16, 32, 128, 384], P('row', 'col')
The draws below stay inside these ranges and needn't reach their ends.
Inputs may be any that keep to these rules, and one draw needn't show every extreme that they name: `near_source`: the 9 slots of a leaf name the nine neighbourhood cells once each. Only the first near_count slots of a leaf are live. `distant_region_list`: each region's list names every region once.
All inputs are finite; a program needn't handle non-finite values.
Results may differ from the reference program's by a relative error of at most 0.013.
Values may be sent and summed in bfloat16 or wider, within the bound.
No kernel may reach another device: no remote copies, remote signals or barrier semaphores. Data moves between devices by JAX's collectives and lax.ppermute only.
A program may use at most 64 MiB of HBM per device.

```python
import jax
import jax.numpy as jnp
from jax import lax

LEAF = 384
RANK = 64
NEAR = 9
VECS = 128
RFAR = 13
BAND = 29
N_ROW = 16
N_COL = 32


def touch_ends(array, key, least, high):
    place = [jax.random.randint(jax.random.fold_in(key, axis), (), 0, length) for axis, length in enumerate(array.shape)]
    main_axis = array.shape.index(max(array.shape))
    next_to = place[:main_axis] + [(place[main_axis] + 1) % array.shape[main_axis]] + place[main_axis + 1:]
    return array.at[tuple(place)].set(least).at[tuple(next_to)].set(high)


def steps_of(key, dims, shards, low, largest):
    level, own = 1.0, jax.random.fold_in(key, 6)
    for axis_at, shards_of in shards:
        heights = jnp.exp(jax.random.uniform(jax.random.fold_in(own, axis_at), (shards_of,), jnp.float32, low / len(shards), largest / len(shards)))
        level = level * jnp.repeat(heights, dims[axis_at] // shards_of).reshape([-1 if axis == axis_at else 1 for axis in range(len(dims))])
    return level


def normal_values(key, extent, width, limit, cuts=(), kind=jnp.bfloat16):
    values = width * jax.random.normal(key, extent, jnp.float32)
    if cuts:
        values = values * steps_of(key, extent, cuts, -0.22, 0.18)
    return jnp.clip(values, -limit, limit).astype(kind)


def setup_inputs(seed: int = 0) -> dict:
    splits = jax.random.split(jax.random.key(seed), 12)
    return {
        "vectors": normal_values(splits[0], (N_ROW, N_COL, VECS, LEAF), 1.0, 6.0, ((0, 16), (1, 32))),
        "near_blocks": normal_values(splits[1], (N_ROW, N_COL, NEAR, LEAF, LEAF), (LEAF * 4) ** -0.5, 0.15625, ((0, 16), (1, 32))),
        "near_source": jax.vmap(lambda own: jax.random.permutation(own, NEAR))(jax.random.split(splits[2], N_ROW * N_COL)).reshape((N_ROW, N_COL, NEAR)).astype(jnp.int32),
        "near_count": touch_ends(jax.random.randint(splits[3], (N_ROW, N_COL), 1, NEAR + 1), jax.random.fold_in(splits[3], 1), 1, NEAR).astype(jnp.int32),
        "basis_col": normal_values(splits[4], (N_ROW, N_COL, RANK, LEAF), LEAF ** -0.5, 0.3125, ((0, 16), (1, 32))),
        "transfer_col": normal_values(splits[5], (N_ROW, N_COL, RANK, RANK), (RANK * N_COL) ** -0.5, 0.125, ((0, 16), (1, 32))),
        "leaf_couple": normal_values(splits[6], (N_ROW, N_COL, 3, BAND, RANK, RANK), (RANK * 3 * BAND) ** -0.5, 0.078125, ((0, 16), (1, 32))),
        "coupling": normal_values(splits[7], (N_ROW, N_ROW, RANK, RANK), (RANK * RFAR) ** -0.5, 0.21875, ((0, 16),)),
        "distant_region_list": jax.vmap(lambda own: jax.random.permutation(own, N_ROW))(jax.random.split(splits[8], N_ROW)).reshape((N_ROW, N_ROW)).astype(jnp.int32),
        "transfer_row": normal_values(splits[9], (N_ROW, N_COL, RANK, RANK), RANK ** -0.5, 0.75, ((0, 16), (1, 32))),
        "basis_row": normal_values(splits[10], (N_ROW, N_COL, RANK, LEAF), RANK ** -0.5, 0.75, ((0, 16), (1, 32))),
    }


def reference(vectors, near_blocks, near_source, near_count, basis_col, transfer_col, leaf_couple, coupling, distant_region_list, transfer_row, basis_row):
    upper_limit = lax.Precision.HIGHEST
    flat_vectors = vectors.reshape(N_ROW * N_COL, VECS, LEAF)
    row_identifiers = jnp.arange(N_ROW, dtype=jnp.int32)[:, None]
    col_ids = jnp.arange(N_COL, dtype=jnp.int32)[None, :]
    near = jnp.zeros((N_ROW, N_COL, VECS, LEAF), jnp.float32)
    for slot in range(NEAR):
        cell = near_source[:, :, slot]
        rows_src = (row_identifiers + cell // 3) % N_ROW
        cols_src = (col_ids + cell % 3) % N_COL
        flat = (rows_src * N_COL + cols_src).astype(jnp.int32)
        source = flat_vectors[flat].astype(jnp.float32)
        live = (near_count > slot).astype(jnp.float32)
        term = jnp.einsum("rcvp,rcpq->rcvq", source, near_blocks[:, :, slot].astype(jnp.float32), precision=upper_limit)
        near = near + live[:, :, None, None] * term
    incoming_leaf = jnp.einsum("rcvp,rckp->rcvk", vectors.astype(jnp.float32), basis_col.astype(jnp.float32), precision=upper_limit)
    band = jnp.zeros((N_ROW, N_COL, VECS, RANK), jnp.float32)
    for delta in range(3):
        for start_shift in range(BAND):
            shifted = jnp.roll(incoming_leaf, (-delta, -(3 + start_shift)), axis=(0, 1))
            band = band + jnp.einsum("rcvk,rckl->rcvl", shifted, leaf_couple[:, :, delta, start_shift].astype(jnp.float32), precision=upper_limit)
    incoming_region = jnp.einsum("rcvk,rckl->rvl", incoming_leaf, transfer_col.astype(jnp.float32), precision=upper_limit)
    region_ids = jnp.arange(N_ROW, dtype=jnp.int32)[:, None]
    far_mask = (((distant_region_list - region_ids) % N_ROW) >= 3).astype(jnp.float32)
    listed = incoming_region[distant_region_list] * far_mask[:, :, None, None]
    outgoing_region = jnp.einsum("ibne,iber->inr", listed, coupling.astype(jnp.float32), precision=upper_limit)
    leaf_out = band + jnp.einsum("rvk,rckl->rcvl", outgoing_region, transfer_row.astype(jnp.float32), precision=upper_limit)
    far = jnp.einsum("rcvk,rckq->rcvq", leaf_out, basis_row.astype(jnp.float32), precision=upper_limit)
    return (near + far).astype(jnp.bfloat16)
```

```python
import jax
import jax.numpy as jnp
from jax import lax
from jax.experimental import pallas as pl
from jax.experimental.pallas import tpu as pltpu
from jax.sharding import PartitionSpec as P

VMEM = pltpu.VMEM
SMEM = pltpu.SMEM
HALF_BAND = 15


def shifted(value, axis, steps):
    count = lax.axis_size(axis)
    return lax.ppermute(value, axis, [((i + steps) % count, i) for i in range(count)])


def contract_rows(left, right):
    return lax.dot_general(left, right, (((0,), (0,)), ((), ())), preferred_element_type=jnp.float32)


def exact_rows(left, right):
    high = right.astype(jnp.bfloat16)
    low = (right - high.astype(jnp.float32)).astype(jnp.bfloat16)
    return contract_rows(left, high) + contract_rows(left, low)


def leaf_kernel(vectors, basis, transfer, out):
    coeff = lax.dot_general(
        basis[0, 0], vectors[0, 0], (((1,), (1,)), ((), ())), preferred_element_type=jnp.float32
    ).astype(jnp.bfloat16)
    half = transfer.shape[2] // 2
    packed = jnp.concatenate([transfer[0, 0, :half], transfer[0, 0, half:]], axis=1)
    chunk = jnp.concatenate([coeff, packed], axis=0)
    for i in range(out.shape[0]):
        out[i] = chunk


def pack_kernel(first, second, out_first, out_second):
    for source, out in ((first, out_first), (second, out_second)):
        bands, rank = source.shape[3], source.shape[4]
        left = source[0, 0, 0, :HALF_BAND].reshape(HALF_BAND * rank, rank)
        right = source[0, 0, 0, HALF_BAND:].reshape((bands - HALF_BAND) * rank, rank)
        right = jnp.concatenate([right, jnp.zeros(((2 * HALF_BAND - bands) * rank, rank), right.dtype)], axis=0)
        out[...] = jnp.concatenate([left, right], axis=1)


def mid_kernel(place, gathered, own, first, second, out, turned):
    row, col = place[0], place[1]
    cols, rank = gathered.shape[0], own.shape[4]
    rows = out.shape[0]
    bands = own.shape[3]
    for j in range(cols):
        turned[j * rank : (j + 1) * rank] = gathered[lax.rem(col + 3 + j, cols), :rank]
    half = rank // 2
    low = gathered[:, :half].reshape(cols * half, -1)
    high = gathered[:, half:rank].reshape(cols * half, -1)
    packed = gathered[:, rank:].reshape(cols * half, -1)
    region = contract_rows(packed[:, :rank], low) + contract_rows(packed[:, rank:], high)
    region = region.astype(out.dtype)
    for a in range(rows):
        out[a] = region
    out[row] = contract_rows(own[0, 0, 0].reshape(bands * rank, rank), turned[: bands * rank]).astype(out.dtype)
    size = HALF_BAND * rank
    for d, weights in ((1, first), (2, second)):
        term = contract_rows(weights[:, :rank], turned[:size]) + contract_rows(
            weights[:, rank:], turned[size : 2 * size]
        )
        out[lax.rem(row + rows - d, rows)] = term.astype(out.dtype)


def near_kernel(source, count, blocks, here, one, two, out, slot_of):
    slots = blocks.shape[2]
    for s in range(slots):
        slot_of[source[0, 0, s]] = s
    live_count = count[0, 0]
    out[...] = jnp.zeros_like(out)
    for cell in range(slots):
        bundle = (here, one, two)[cell // 3]
        slot = slot_of[cell]

        @pl.when(slot < live_count)
        def _():
            out[...] += jnp.dot(bundle[cell % 3], blocks[0, 0, slot], preferred_element_type=jnp.float32)


def final_kernel(place, listing, received, coupling, transfer, basis, near, out, terms):
    row = place[0]
    rows, rank = received.shape[0], received.shape[1]
    band = jnp.zeros(received.shape[1:], jnp.float32)
    for f in range(rows):
        region = listing[0, f]
        part = received[region]
        is_far = lax.rem(region - row + rows, rows) >= 3
        terms[f * rank : (f + 1) * rank] = jnp.where(is_far, part, jnp.zeros_like(part))
        band += jnp.where(is_far, jnp.zeros_like(part), part).astype(jnp.float32)
    outgoing = contract_rows(coupling[0].reshape(rows * rank, rank), terms[...])
    leaf_out = band + exact_rows(transfer[0, 0], outgoing)
    high = leaf_out.astype(jnp.bfloat16)
    low = (leaf_out - high.astype(jnp.float32)).astype(jnp.bfloat16)
    far = contract_rows(high, basis[0, 0]) + contract_rows(low, basis[0, 0])
    out[0, 0] = (near[...] + far).astype(out.dtype)


def call(kernel, out_shape, in_specs, scratch, cost, name):
    return pl.pallas_call(
        kernel,
        out_shape=out_shape,
        in_specs=in_specs,
        out_specs=jax.tree.map(lambda _: pl.BlockSpec(memory_space=VMEM), out_shape),
        scratch_shapes=scratch,
        cost_estimate=pl.CostEstimate(flops=cost[0], bytes_accessed=cost[1], transcendentals=0),
        compiler_params=pltpu.CompilerParams(vmem_limit_bytes=24 * 1024 * 1024),
        name=name,
    )


def per_device(
    vectors,
    near_blocks,
    near_source,
    near_count,
    basis_col,
    transfer_col,
    leaf_couple,
    coupling,
    distant_region_list,
    transfer_row,
    basis_row,
):
    rows, cols = lax.axis_size("row"), lax.axis_size("col")
    vecs, leaf = vectors.shape[2:]
    rank = basis_col.shape[2]
    bands = leaf_couple.shape[3]
    bf16, f32 = jnp.bfloat16, jnp.float32
    vmem, smem = pl.BlockSpec(memory_space=VMEM), pl.BlockSpec(memory_space=SMEM)
    place = jnp.stack([lax.axis_index("row"), lax.axis_index("col")]).astype(jnp.int32)

    col_one = shifted(vectors[0, 0], "col", 1)
    col_two = shifted(vectors[0, 0], "col", 2)

    chunks = call(
        leaf_kernel,
        jax.ShapeDtypeStruct((cols, rank + rank // 2, vecs), bf16),
        [vmem] * 3,
        [],
        (2 * rank * vecs * leaf, 2 * cols * 96 * vecs),
        "leaf",
    )(vectors, basis_col, transfer_col)
    gathered = lax.all_to_all(chunks, "col", split_axis=0, concat_axis=0, tiled=True)

    def slab(d):
        return pl.BlockSpec((1, 1, 1, bands, rank, rank), lambda i: (0, 0, d, 0, 0, 0))

    packed_shape = jax.ShapeDtypeStruct((HALF_BAND * rank, 2 * rank), bf16)
    first, second = pl.pallas_call(
        pack_kernel,
        grid=(1,),
        out_shape=[packed_shape] * 2,
        in_specs=[slab(1), slab(2)],
        out_specs=[pl.BlockSpec(packed_shape.shape, lambda i: (0, 0))] * 2,
        cost_estimate=pl.CostEstimate(flops=0, bytes_accessed=2000000, transcendentals=0),
        name="pack",
    )(leaf_couple, leaf_couple)
    first = shifted(first, "row", -1)
    second = shifted(second, "row", -2)

    here = jnp.stack([vectors[0, 0], col_one, col_two])
    row_one = shifted(here, "row", 1)
    row_two = shifted(here, "row", 2)

    outgoing = pl.pallas_call(
        mid_kernel,
        grid=(1,),
        out_shape=jax.ShapeDtypeStruct((rows, rank, vecs), bf16),
        in_specs=[
            smem,
            pl.BlockSpec((cols, rank + rank // 2, vecs), lambda i: (0, 0, 0)),
            slab(0),
            pl.BlockSpec(packed_shape.shape, lambda i: (0, 0)),
            pl.BlockSpec(packed_shape.shape, lambda i: (0, 0)),
        ],
        out_specs=pl.BlockSpec((rows, rank, vecs), lambda i: (0, 0, 0)),
        scratch_shapes=[VMEM((cols * rank, vecs), bf16)],
        cost_estimate=pl.CostEstimate(flops=2 * 2048 * 256 * 128, bytes_accessed=3000000, transcendentals=0),
        compiler_params=pltpu.CompilerParams(vmem_limit_bytes=24 * 1024 * 1024),
        name="mid",
    )(place, gathered, leaf_couple, first, second)
    received = lax.all_to_all(outgoing, "row", split_axis=0, concat_axis=0, tiled=True)

    near = call(
        near_kernel,
        jax.ShapeDtypeStruct((vecs, leaf), f32),
        [smem, smem, vmem, vmem, vmem, vmem],
        [SMEM((near_blocks.shape[2],), jnp.int32)],
        (2 * 9 * vecs * leaf * leaf, 2 * 9 * leaf * (leaf + vecs)),
        "near",
    )(near_source, near_count, near_blocks, here, row_one, row_two)

    return call(
        final_kernel,
        jax.ShapeDtypeStruct((1, 1, vecs, leaf), bf16),
        [smem, smem, vmem, vmem, vmem, vmem, vmem],
        [VMEM((rows * rank, vecs), bf16)],
        (2 * 1024 * 64 * 128 + 4 * 64 * 128 * 384, 1000000),
        "final",
    )(place, distant_region_list, received, coupling, transfer_row, basis_row, near)


def solution(mesh):
    placed = (
        P("row", "col", None, None),
        P("row", "col", None, None, None),
        P("row", "col", None),
        P("row", "col"),
        P("row", "col", None, None),
        P("row", "col", None, None),
        P("row", "col", None, None, None, None),
        P("row", None, None, None),
        P("row", None),
        P("row", "col", None, None),
        P("row", "col", None, None),
    )
    return jax.shard_map(
        per_device,
        mesh=mesh,
        in_specs=placed,
        out_specs=P("row", "col", None, None),
        check_vma=False,
    )
```

```python
import jax
import jax.numpy as jnp
from jax import lax
from jax.experimental import pallas as pl
from jax.experimental.pallas import tpu as pltpu
from jax.sharding import PartitionSpec as P

VMEM = pltpu.VMEM
SMEM = pltpu.SMEM
VL = 8
LINES = 8
HALF_BAND = 15


def shifted(value, axis, steps):
    count = lax.axis_size(axis)
    return lax.ppermute(value, axis, [((i + steps) % count, i) for i in range(count)])


def contract_rows(left, right):
    return lax.dot_general(left, right, (((0,), (0,)), ((), ())), preferred_element_type=jnp.float32)


def exact_rows(left, right):
    high = right.astype(jnp.bfloat16)
    low = (right - high.astype(jnp.float32)).astype(jnp.bfloat16)
    return contract_rows(left, high) + contract_rows(left, low)


def leaf_kernel(vectors, basis, transfer, out):
    coeff = lax.dot_general(
        basis[0, 0], vectors[0, 0], (((1,), (1,)), ((), ())), preferred_element_type=jnp.float32
    ).astype(jnp.bfloat16)
    half = transfer.shape[2] // 2
    packed = jnp.concatenate([transfer[0, 0, :half], transfer[0, 0, half:]], axis=1)
    chunk = jnp.concatenate([coeff, packed], axis=0)
    for i in range(out.shape[0]):
        out[i] = chunk


def fold_kernel(gathered, out):
    lines, depth = gathered.shape[0], gathered.shape[1]
    rank = 2 * depth // 3
    half = rank // 2
    low = gathered[:, :half].reshape(lines * half, -1)
    high = gathered[:, half:rank].reshape(lines * half, -1)
    packed = gathered[:, rank:].reshape(lines * half, -1)
    region = contract_rows(packed[:, :rank], low) + contract_rows(packed[:, rank:], high)
    leaves = gathered[:, :rank].reshape(lines * rank, -1)
    chunk = jnp.concatenate([leaves, region.astype(out.dtype)], axis=0)
    for i in range(out.shape[0]):
        out[i] = chunk


def pack_kernel(first, second, out_first, out_second):
    for source, out in ((first, out_first), (second, out_second)):
        bands, rank = source.shape[3], source.shape[4]
        left = source[0, 0, 0, :HALF_BAND].reshape(HALF_BAND * rank, rank)
        right = source[0, 0, 0, HALF_BAND:].reshape((bands - HALF_BAND) * rank, rank)
        right = jnp.concatenate([right, jnp.zeros(((2 * HALF_BAND - bands) * rank, rank), right.dtype)], axis=0)
        out[...] = jnp.concatenate([left, right], axis=1)


def mid_kernel(place, gathered, own, first, second, out, turned):
    row, col = place[0], place[1]
    bands, rank = own.shape[3], own.shape[4]
    groups, lines = gathered.shape[0], gathered.shape[1] // rank - 1
    cols, rows = groups * lines, out.shape[0]
    for j in range(cols):
        source = lax.rem(col + 3 + j, cols)
        start = pl.multiple_of(lax.rem(source, lines) * rank, rank)
        turned[j * rank : (j + 1) * rank] = gathered[source // lines, pl.ds(start, rank)]
    region = sum(gathered[x, lines * rank :].astype(jnp.float32) for x in range(groups)).astype(out.dtype)
    for a in range(rows):
        out[a] = region
    out[row] = contract_rows(own[0, 0, 0].reshape(bands * rank, rank), turned[: bands * rank]).astype(out.dtype)
    size = HALF_BAND * rank
    for d, weights in ((1, first), (2, second)):
        term = contract_rows(weights[:, :rank], turned[:size]) + contract_rows(
            weights[:, rank:], turned[size : 2 * size]
        )
        out[lax.rem(row + rows - d, rows)] = term.astype(out.dtype)


def near_kernel(source, count, blocks, here, one, two, out, slot_of):
    slots = blocks.shape[2]
    for s in range(slots):
        slot_of[source[0, 0, s]] = s
    live_count = count[0, 0]
    out[...] = jnp.zeros_like(out)
    for cell in range(slots):
        bundle = (here, one, two)[cell // 3]
        slot = slot_of[cell]

        @pl.when(slot < live_count)
        def _():
            out[...] += jnp.dot(bundle[cell % 3], blocks[0, 0, slot], preferred_element_type=jnp.float32)


def final_kernel(place, listing, received, coupling, transfer, basis, near, out, terms):
    row = place[0]
    rows, rank = received.shape[0], received.shape[1]
    band = jnp.zeros(received.shape[1:], jnp.float32)
    for f in range(rows):
        region = listing[0, f]
        part = received[region]
        is_far = lax.rem(region - row + rows, rows) >= 3
        terms[f * rank : (f + 1) * rank] = jnp.where(is_far, part, jnp.zeros_like(part))
        band += jnp.where(is_far, jnp.zeros_like(part), part).astype(jnp.float32)
    outgoing = contract_rows(coupling[0].reshape(rows * rank, rank), terms[...])
    leaf_out = band + exact_rows(transfer[0, 0], outgoing)
    high = leaf_out.astype(jnp.bfloat16)
    low = (leaf_out - high.astype(jnp.float32)).astype(jnp.bfloat16)
    far = contract_rows(high, basis[0, 0]) + contract_rows(low, basis[0, 0])
    out[0, 0] = (near[...] + far).astype(out.dtype)


def whole(shape):
    return pl.BlockSpec(shape, lambda i: (0,) * len(shape))


def call(kernel, out_shape, in_specs, scratch, cost, name):
    return pl.pallas_call(
        kernel,
        out_shape=out_shape,
        in_specs=in_specs,
        out_specs=jax.tree.map(lambda _: pl.BlockSpec(memory_space=VMEM), out_shape),
        scratch_shapes=scratch,
        cost_estimate=pl.CostEstimate(flops=cost[0], bytes_accessed=cost[1], transcendentals=0),
        compiler_params=pltpu.CompilerParams(vmem_limit_bytes=VL * 1024 * 1024),
        name=name,
    )


def per_device(
    vectors,
    near_blocks,
    near_source,
    near_count,
    basis_col,
    transfer_col,
    leaf_couple,
    coupling,
    distant_region_list,
    transfer_row,
    basis_row,
):
    rows, cols = lax.axis_size("row"), lax.axis_size("col")
    vecs, leaf = vectors.shape[2:]
    rank = basis_col.shape[2]
    bands = leaf_couple.shape[3]
    bf16, f32 = jnp.bfloat16, jnp.float32
    vmem, smem = pl.BlockSpec(memory_space=VMEM), pl.BlockSpec(memory_space=SMEM)
    place = jnp.stack([lax.axis_index("row"), lax.axis_index("col")]).astype(jnp.int32)

    col_one = shifted(vectors[0, 0], "col", 1)
    col_two = shifted(vectors[0, 0], "col", 2)

    chunk_shape = (LINES, rank + rank // 2, vecs)
    groups = cols // LINES
    chunks = pl.pallas_call(
        leaf_kernel,
        grid=(1,),
        out_shape=jax.ShapeDtypeStruct(chunk_shape, bf16),
        in_specs=[whole(a.shape) for a in (vectors, basis_col, transfer_col)],
        out_specs=whole(chunk_shape),
        cost_estimate=pl.CostEstimate(flops=2 * rank * vecs * leaf, bytes_accessed=1000000, transcendentals=0),
        name="leaf",
    )(vectors, basis_col, transfer_col)
    near_cols = [[x * LINES + z for z in range(LINES)] for x in range(groups)]
    far_cols = [[x * LINES + z for x in range(groups)] for z in range(LINES)]
    line = lax.all_to_all(chunks, "col", 0, 0, axis_index_groups=near_cols, tiled=True)
    folded_shape = (groups, (LINES + 1) * rank, vecs)
    folded = pl.pallas_call(
        fold_kernel,
        grid=(1,),
        out_shape=jax.ShapeDtypeStruct(folded_shape, bf16),
        in_specs=[whole(chunk_shape)],
        out_specs=whole(folded_shape),
        cost_estimate=pl.CostEstimate(flops=2 * LINES * rank * rank * vecs, bytes_accessed=1000000, transcendentals=0),
        name="fold",
    )(line)
    gathered = lax.all_to_all(folded, "col", 0, 0, axis_index_groups=far_cols, tiled=True)

    def slab(d):
        return pl.BlockSpec((1, 1, 1, bands, rank, rank), lambda i: (0, 0, d, 0, 0, 0))

    packed_shape = jax.ShapeDtypeStruct((HALF_BAND * rank, 2 * rank), bf16)
    packed_one, packed_two = pl.pallas_call(
        pack_kernel,
        grid=(1,),
        out_shape=[packed_shape] * 2,
        in_specs=[slab(1), slab(2)],
        out_specs=[pl.BlockSpec(packed_shape.shape, lambda i: (0, 0))] * 2,
        cost_estimate=pl.CostEstimate(flops=0, bytes_accessed=2000000, transcendentals=0),
        name="pack",
    )(leaf_couple, leaf_couple)
    first = shifted(packed_one, "row", -1)
    second = shifted(packed_two, "row", -2)

    col_one, first, second = lax.optimization_barrier((col_one, first, second))
    here = jnp.stack([vectors[0, 0], col_one, col_two])
    row_one = shifted(here, "row", 1)
    row_two = shifted(here, "row", 2)

    leaf_couple, here = lax.optimization_barrier((leaf_couple, here))
    outgoing = pl.pallas_call(
        mid_kernel,
        grid=(1,),
        out_shape=jax.ShapeDtypeStruct((rows, rank, vecs), bf16),
        in_specs=[
            smem,
            whole(folded_shape),
            slab(0),
            pl.BlockSpec(packed_shape.shape, lambda i: (0, 0)),
            pl.BlockSpec(packed_shape.shape, lambda i: (0, 0)),
        ],
        out_specs=pl.BlockSpec((rows, rank, vecs), lambda i: (0, 0, 0)),
        scratch_shapes=[VMEM((cols * rank, vecs), bf16)],
        cost_estimate=pl.CostEstimate(flops=2 * 2048 * 256 * 128, bytes_accessed=3000000, transcendentals=0),
        compiler_params=pltpu.CompilerParams(vmem_limit_bytes=VL * 1024 * 1024),
        name="mid",
    )(place, gathered, leaf_couple, first, second)
    received = lax.all_to_all(outgoing, "row", split_axis=0, concat_axis=0, tiled=True)

    near = call(
        near_kernel,
        jax.ShapeDtypeStruct((vecs, leaf), f32),
        [smem, smem, vmem, vmem, vmem, vmem],
        [SMEM((near_blocks.shape[2],), jnp.int32)],
        (2**36, 2 * 9 * leaf * (leaf + vecs)),
        "near",
    )(near_source, near_count, near_blocks, here, row_one, row_two)

    return call(
        final_kernel,
        jax.ShapeDtypeStruct((1, 1, vecs, leaf), bf16),
        [smem, smem, vmem, vmem, vmem, vmem, vmem],
        [VMEM((rows * rank, vecs), bf16)],
        (2 * 1024 * 64 * 128 + 4 * 64 * 128 * 384, 1000000),
        "final",
    )(place, distant_region_list, received, coupling, transfer_row, basis_row, near)


def solution(mesh):
    placed = (
        P("row", "col", None, None),
        P("row", "col", None, None, None),
        P("row", "col", None),
        P("row", "col"),
        P("row", "col", None, None),
        P("row", "col", None, None),
        P("row", "col", None, None, None, None),
        P("row", None, None, None),
        P("row", None),
        P("row", "col", None, None),
        P("row", "col", None, None),
    )
    return jax.shard_map(
        per_device,
        mesh=mesh,
        in_specs=placed,
        out_specs=P("row", "col", None, None),
        check_vma=False,
    )
```

```python
import jax
import jax.numpy as jnp
from jax import lax
from jax.experimental import pallas as pl
from jax.experimental.pallas import tpu as pltpu
from jax.sharding import PartitionSpec as P

VMEM = pltpu.VMEM
SMEM = pltpu.SMEM
VL = 8
LINES = 8
HALF_BAND = 15


def shifted(value, axis, steps):
    count = lax.axis_size(axis)
    return lax.ppermute(value, axis, [((i + steps) % count, i) for i in range(count)])


def contract_rows(left, right):
    return lax.dot_general(left, right, (((0,), (0,)), ((), ())), preferred_element_type=jnp.float32)


def exact_rows(left, right):
    high = right.astype(jnp.bfloat16)
    low = (right - high.astype(jnp.float32)).astype(jnp.bfloat16)
    return contract_rows(left, high) + contract_rows(left, low)


def leaf_kernel(vectors, basis, transfer, out):
    coeff = lax.dot_general(
        basis[0, 0], vectors[0, 0], (((1,), (1,)), ((), ())), preferred_element_type=jnp.float32
    ).astype(jnp.bfloat16)
    half = transfer.shape[2] // 2
    packed = jnp.concatenate([transfer[0, 0, :half], transfer[0, 0, half:]], axis=1)
    chunk = jnp.concatenate([coeff, packed], axis=0)
    for i in range(out.shape[0]):
        out[i] = chunk


def fold_kernel(gathered, out):
    lines, depth = gathered.shape[0], gathered.shape[1]
    rank = 2 * depth // 3
    half = rank // 2
    low = gathered[:, :half].reshape(lines * half, -1)
    high = gathered[:, half:rank].reshape(lines * half, -1)
    packed = gathered[:, rank:].reshape(lines * half, -1)
    region = contract_rows(packed[:, :rank], low) + contract_rows(packed[:, rank:], high)
    leaves = gathered[:, :rank].reshape(lines * rank, -1)
    chunk = jnp.concatenate([leaves, region.astype(out.dtype)], axis=0)
    for i in range(out.shape[0]):
        out[i] = chunk


def pack_kernel(couple, out_first, out_second):
    bands, rank = couple.shape[3], couple.shape[4]
    size = HALF_BAND * rank
    rest = (bands - HALF_BAND) * rank
    for d, out in ((1, out_first), (2, out_second)):
        out[:, :rank] = couple[0, 0, d, :HALF_BAND].reshape(size, rank)
        out[:rest, rank:] = couple[0, 0, d, HALF_BAND:].reshape(rest, rank)
        out[rest:, rank:] = jnp.zeros((size - rest, rank), out.dtype)


def mid_kernel(gathered, own, first, second, out, turned):
    row, col = lax.axis_index("row"), lax.axis_index("col")
    bands, rank = own.shape[3], own.shape[4]
    groups, lines = gathered.shape[0], gathered.shape[1] // rank - 1
    cols, rows = groups * lines, out.shape[0]
    for j in range(cols):
        source = lax.rem(col + 3 + j, cols)
        start = pl.multiple_of(lax.rem(source, lines) * rank, rank)
        turned[j * rank : (j + 1) * rank] = gathered[source // lines, pl.ds(start, rank)]
    region = sum(gathered[x, lines * rank :].astype(jnp.float32) for x in range(groups)).astype(out.dtype)
    for a in range(rows):
        out[a] = region
    out[row] = contract_rows(own[0, 0, 0].reshape(bands * rank, rank), turned[: bands * rank]).astype(out.dtype)
    size = HALF_BAND * rank
    both = jnp.concatenate([first[...], second[...]], axis=1)
    low = contract_rows(both, turned[:size])
    high = contract_rows(both, turned[size : 2 * size])
    for d in (1, 2):
        start = 2 * (d - 1) * rank
        term = low[start : start + rank] + high[start + rank : start + 2 * rank]
        out[lax.rem(row + rows - d, rows)] = term.astype(out.dtype)


def near_kernel(source, count, listing, blocks, here, one, two, coupling, out, ordered, slot_of):
    slots = blocks.shape[2]
    rows = coupling.shape[1]
    row = lax.axis_index("row")
    for f in range(rows):
        region = listing[0, f]
        is_far = lax.rem(region - row + rows, rows) >= 3
        ordered[region] = jnp.where(is_far, coupling[0, f], jnp.zeros_like(coupling[0, f]))
    for s in range(slots):
        slot_of[source[0, 0, s]] = s
    live_count = count[0, 0]
    out[...] = jnp.zeros_like(out)
    for cell in range(slots):
        bundle = (here, one, two)[cell // 3]
        slot = slot_of[cell]

        @pl.when(slot < live_count)
        def _():
            out[...] += jnp.dot(bundle[cell % 3], blocks[0, 0, slot], preferred_element_type=jnp.float32)


def final_kernel(received, ordered, transfer, basis, near, out):
    row = lax.axis_index("row")
    rows, rank = received.shape[0], received.shape[1]
    band = received[row].astype(jnp.float32)
    for d in (1, 2):
        band += received[lax.rem(row + d, rows)].astype(jnp.float32)
    outgoing = contract_rows(
        ordered[...].reshape(rows * rank, rank), received[...].reshape(rows * rank, received.shape[2])
    )
    leaf_out = band + exact_rows(transfer[0, 0], outgoing)
    high = leaf_out.astype(jnp.bfloat16)
    low = (leaf_out - high.astype(jnp.float32)).astype(jnp.bfloat16)
    far = contract_rows(high, basis[0, 0]) + contract_rows(low, basis[0, 0])
    out[0, 0] = (near[...] + far).astype(out.dtype)


def whole(shape):
    return pl.BlockSpec(shape, lambda i: (0,) * len(shape))


def call(kernel, out_shape, in_specs, scratch, cost, name):
    return pl.pallas_call(
        kernel,
        out_shape=out_shape,
        in_specs=in_specs,
        out_specs=jax.tree.map(lambda _: pl.BlockSpec(memory_space=VMEM), out_shape),
        scratch_shapes=scratch,
        cost_estimate=pl.CostEstimate(flops=cost[0], bytes_accessed=cost[1], transcendentals=0),
        compiler_params=pltpu.CompilerParams(vmem_limit_bytes=VL * 1024 * 1024),
        name=name,
    )


def per_device(
    vectors,
    near_blocks,
    near_source,
    near_count,
    basis_col,
    transfer_col,
    leaf_couple,
    coupling,
    distant_region_list,
    transfer_row,
    basis_row,
):
    rows, cols = lax.axis_size("row"), lax.axis_size("col")
    vecs, leaf = vectors.shape[2:]
    rank = basis_col.shape[2]
    bands = leaf_couple.shape[3]
    bf16, f32 = jnp.bfloat16, jnp.float32
    vmem, smem = pl.BlockSpec(memory_space=VMEM), pl.BlockSpec(memory_space=SMEM)

    col_one = shifted(vectors[0, 0], "col", 1)
    col_two = shifted(vectors[0, 0], "col", 2)

    chunk_shape = (LINES, rank + rank // 2, vecs)
    groups = cols // LINES
    chunks = pl.pallas_call(
        leaf_kernel,
        grid=(1,),
        out_shape=jax.ShapeDtypeStruct(chunk_shape, bf16),
        in_specs=[whole(a.shape) for a in (vectors, basis_col, transfer_col)],
        out_specs=whole(chunk_shape),
        cost_estimate=pl.CostEstimate(flops=2 * rank * vecs * leaf, bytes_accessed=1000000, transcendentals=0),
        name="leaf",
    )(vectors, basis_col, transfer_col)
    near_cols = [[x * LINES + z for z in range(LINES)] for x in range(groups)]
    far_cols = [[x * LINES + z for x in range(groups)] for z in range(LINES)]
    line = lax.all_to_all(chunks, "col", 0, 0, axis_index_groups=near_cols, tiled=True)
    folded_shape = (groups, (LINES + 1) * rank, vecs)
    folded = call(
        fold_kernel,
        jax.ShapeDtypeStruct(folded_shape, bf16),
        [vmem],
        [],
        (2 * LINES * rank * rank * vecs, 1000000),
        "fold",
    )(line)
    gathered = lax.all_to_all(folded, "col", 0, 0, axis_index_groups=far_cols, tiled=True)

    packed_shape = jax.ShapeDtypeStruct((HALF_BAND * rank, 2 * rank), bf16)
    packed_one, packed_two = call(
        pack_kernel,
        [packed_shape] * 2,
        [vmem],
        [],
        (0, 2000000),
        "pack",
    )(leaf_couple)
    col_one, col_two, packed_one, packed_two = lax.optimization_barrier((col_one, col_two, packed_one, packed_two))
    first = shifted(packed_one, "row", -1)
    second = shifted(packed_two, "row", -2)

    here = jnp.stack([vectors[0, 0], col_one, col_two])
    row_one = shifted(here, "row", 1)
    row_two = shifted(here, "row", 2)

    leaf_couple, here = lax.optimization_barrier((leaf_couple, here))
    outgoing = call(
        mid_kernel,
        jax.ShapeDtypeStruct((rows, rank, vecs), bf16),
        [vmem, vmem, vmem, vmem],
        [VMEM((cols * rank, vecs), bf16)],
        (2**29, 3000000),
        "mid",
    )(gathered, leaf_couple, first, second)
    received = lax.all_to_all(outgoing, "row", split_axis=0, concat_axis=0, tiled=True)

    near, ordered = call(
        near_kernel,
        [jax.ShapeDtypeStruct((vecs, leaf), f32), jax.ShapeDtypeStruct(coupling.shape[1:], bf16)],
        [smem, smem, smem, vmem, vmem, vmem, vmem, vmem],
        [SMEM((near_blocks.shape[2],), jnp.int32)],
        (2**36, 2 * 9 * leaf * (leaf + vecs)),
        "near",
    )(near_source, near_count, distant_region_list, near_blocks, here, row_one, row_two, coupling)

    return call(
        final_kernel,
        jax.ShapeDtypeStruct((1, 1, vecs, leaf), bf16),
        [vmem] * 5,
        [],
        (2 * 1024 * 64 * 128 + 4 * 64 * 128 * 384, 1000000),
        "final",
    )(received, ordered, transfer_row, basis_row, near)


def solution(mesh):
    placed = (
        P("row", "col", None, None),
        P("row", "col", None, None, None),
        P("row", "col", None),
        P("row", "col"),
        P("row", "col", None, None),
        P("row", "col", None, None),
        P("row", "col", None, None, None, None),
        P("row", None, None, None),
        P("row", None),
        P("row", "col", None, None),
        P("row", "col", None, None),
    )
    return jax.shard_map(
        per_device,
        mesh=mesh,
        in_specs=placed,
        out_specs=P("row", "col", None, None),
        check_vma=False,
    )
```

```python
import jax
import jax.numpy as jnp
from jax import lax
from jax.experimental import pallas as pl
from jax.experimental.pallas import tpu as pltpu
from jax.sharding import PartitionSpec as P

VMEM = pltpu.VMEM
SMEM = pltpu.SMEM
VL = 8
LINES = 8
HALF_BAND = 15


def shifted(value, axis, steps):
    count = lax.axis_size(axis)
    return lax.ppermute(value, axis, [((i + steps) % count, i) for i in range(count)])


def contract_rows(left, right):
    return lax.dot_general(left, right, (((0,), (0,)), ((), ())), preferred_element_type=jnp.float32)


def exact_rows(left, right):
    high = right.astype(jnp.bfloat16)
    low = (right - high.astype(jnp.float32)).astype(jnp.bfloat16)
    return contract_rows(left, high) + contract_rows(left, low)


def leaf_kernel(vectors, basis, transfer, out):
    coeff = lax.dot_general(
        basis[0, 0], vectors[0, 0], (((1,), (1,)), ((), ())), preferred_element_type=jnp.float32
    ).astype(jnp.bfloat16)
    half = transfer.shape[2] // 2
    packed = jnp.concatenate([transfer[0, 0, :half], transfer[0, 0, half:]], axis=1)
    chunk = jnp.concatenate([coeff, packed], axis=0)
    for i in range(out.shape[0]):
        out[i] = chunk


def fold_kernel(gathered, out, chunk, sems):
    lines, depth = gathered.shape[0], gathered.shape[1]
    rank = 2 * depth // 3
    half = rank // 2
    size = lines * rank

    def send(part, start, length):
        return [
            pltpu.make_async_copy(
                chunk.at[pl.ds(start, length)], out.at[i, pl.ds(start, length)], sems.at[part, i]
            )
            for i in range(out.shape[0])
        ]

    chunk[:size] = gathered[:, :rank].reshape(size, -1)
    leaves = send(0, 0, size)
    for copy in leaves:
        copy.start()
    low = gathered[:, :half].reshape(lines * half, -1)
    high = gathered[:, half:rank].reshape(lines * half, -1)
    packed = gathered[:, rank:].reshape(lines * half, -1)
    region = contract_rows(packed[:, :rank], low) + contract_rows(packed[:, rank:], high)
    chunk[size:] = region.astype(chunk.dtype)
    regions = send(1, size, rank)
    for copy in regions:
        copy.start()
    for copy in leaves + regions:
        copy.wait()


def pack_kernel(couple, out_first, out_second):
    bands, rank = couple.shape[3], couple.shape[4]
    size = HALF_BAND * rank
    rest = (bands - HALF_BAND) * rank
    for d, out in ((1, out_first), (2, out_second)):
        out[:, :rank] = couple[0, 0, d, :HALF_BAND].reshape(size, rank)
        out[:rest, rank:] = couple[0, 0, d, HALF_BAND:].reshape(rest, rank)
        out[rest:, rank:] = jnp.zeros((size - rest, rank), out.dtype)


def mid_kernel(gathered, own, first, second, out, turned):
    row, col = lax.axis_index("row"), lax.axis_index("col")
    bands, rank = own.shape[3], own.shape[4]
    groups, lines = gathered.shape[0], gathered.shape[1] // rank - 1
    cols, rows = groups * lines, out.shape[0]
    for j in range(cols):
        source = lax.rem(col + 3 + j, cols)
        start = pl.multiple_of(lax.rem(source, lines) * rank, rank)
        turned[j * rank : (j + 1) * rank] = gathered[source // lines, pl.ds(start, rank)]
    region = sum(gathered[x, lines * rank :].astype(jnp.float32) for x in range(groups)).astype(out.dtype)
    for a in range(rows):
        out[a] = region
    out[row] = contract_rows(own[0, 0, 0].reshape(bands * rank, rank), turned[: bands * rank]).astype(out.dtype)
    size = HALF_BAND * rank
    both = jnp.concatenate([first[...], second[...]], axis=1)
    low = contract_rows(both, turned[:size])
    high = contract_rows(both, turned[size : 2 * size])
    for d in (1, 2):
        start = 2 * (d - 1) * rank
        term = low[start : start + rank] + high[start + rank : start + 2 * rank]
        out[lax.rem(row + rows - d, rows)] = term.astype(out.dtype)


def near_kernel(source, count, listing, blocks, here, one, two, coupling, out, ordered, slot_of):
    slots = blocks.shape[2]
    rows = coupling.shape[1]
    row = lax.axis_index("row")
    for f in range(rows):
        region = listing[0, f]
        is_far = lax.rem(region - row + rows, rows) >= 3
        ordered[region] = jnp.where(is_far, coupling[0, f], jnp.zeros_like(coupling[0, f]))
    for s in range(slots):
        slot_of[source[0, 0, s]] = s
    live_count = count[0, 0]
    out[...] = jnp.zeros_like(out)
    for cell in range(slots):
        bundle = (here, one, two)[cell // 3]
        slot = slot_of[cell]

        @pl.when(slot < live_count)
        def _():
            out[...] += jnp.dot(bundle[cell % 3], blocks[0, 0, slot], preferred_element_type=jnp.float32)


def final_kernel(received, ordered, transfer, basis, near, out):
    row = lax.axis_index("row")
    rows, rank = received.shape[0], received.shape[1]
    band = received[row].astype(jnp.float32)
    for d in (1, 2):
        band += received[lax.rem(row + d, rows)].astype(jnp.float32)
    outgoing = contract_rows(
        ordered[...].reshape(rows * rank, rank), received[...].reshape(rows * rank, received.shape[2])
    )
    leaf_out = band + exact_rows(transfer[0, 0], outgoing)
    high = leaf_out.astype(jnp.bfloat16)
    low = (leaf_out - high.astype(jnp.float32)).astype(jnp.bfloat16)
    far = contract_rows(high, basis[0, 0]) + contract_rows(low, basis[0, 0])
    out[0, 0] = (near[...] + far).astype(out.dtype)


def whole(shape):
    return pl.BlockSpec(shape, lambda i: (0,) * len(shape))


def call(kernel, out_shape, in_specs, scratch, cost, name, out_space=VMEM):
    return pl.pallas_call(
        kernel,
        out_shape=out_shape,
        in_specs=in_specs,
        out_specs=jax.tree.map(lambda _: pl.BlockSpec(memory_space=out_space), out_shape),
        scratch_shapes=scratch,
        cost_estimate=pl.CostEstimate(flops=cost[0], bytes_accessed=cost[1], transcendentals=0),
        compiler_params=pltpu.CompilerParams(vmem_limit_bytes=VL * 1024 * 1024),
        name=name,
    )


def per_device(
    vectors,
    near_blocks,
    near_source,
    near_count,
    basis_col,
    transfer_col,
    leaf_couple,
    coupling,
    distant_region_list,
    transfer_row,
    basis_row,
):
    rows, cols = lax.axis_size("row"), lax.axis_size("col")
    vecs, leaf = vectors.shape[2:]
    rank = basis_col.shape[2]
    bands = leaf_couple.shape[3]
    bf16, f32 = jnp.bfloat16, jnp.float32
    vmem, smem = pl.BlockSpec(memory_space=VMEM), pl.BlockSpec(memory_space=SMEM)

    col_one = shifted(vectors[0, 0], "col", 1)
    col_two = shifted(vectors[0, 0], "col", 2)

    chunk_shape = (LINES, rank + rank // 2, vecs)
    groups = cols // LINES
    chunks = pl.pallas_call(
        leaf_kernel,
        grid=(1,),
        out_shape=jax.ShapeDtypeStruct(chunk_shape, bf16),
        in_specs=[whole(a.shape) for a in (vectors, basis_col, transfer_col)],
        out_specs=whole(chunk_shape),
        cost_estimate=pl.CostEstimate(flops=2 * rank * vecs * leaf, bytes_accessed=1000000, transcendentals=0),
        name="leaf",
    )(vectors, basis_col, transfer_col)
    near_cols = [[x * LINES + z for z in range(LINES)] for x in range(groups)]
    far_cols = [[x * LINES + z for x in range(groups)] for z in range(LINES)]
    line = lax.all_to_all(chunks, "col", 0, 0, axis_index_groups=near_cols, tiled=True)
    folded_shape = (groups, (LINES + 1) * rank, vecs)
    folded = call(
        fold_kernel,
        jax.ShapeDtypeStruct(folded_shape, bf16),
        [vmem],
        [VMEM(folded_shape[1:], bf16), pltpu.SemaphoreType.DMA((2, groups))],
        (2 * LINES * rank * rank * vecs, 1000000),
        "fold",
        pl.ANY,
    )(line)
    gathered = lax.all_to_all(folded, "col", 0, 0, axis_index_groups=far_cols, tiled=True)

    packed_shape = jax.ShapeDtypeStruct((HALF_BAND * rank, 2 * rank), bf16)
    packed_one, packed_two = call(
        pack_kernel,
        [packed_shape] * 2,
        [vmem],
        [],
        (0, 2000000),
        "pack",
    )(leaf_couple)
    col_one, col_two, packed_one, packed_two = lax.optimization_barrier((col_one, col_two, packed_one, packed_two))
    first = shifted(packed_one, "row", -1)
    second = shifted(packed_two, "row", -2)

    here = jnp.stack([vectors[0, 0], col_one, col_two])
    row_one = shifted(here, "row", 1)
    row_two = shifted(here, "row", 2)

    leaf_couple, here = lax.optimization_barrier((leaf_couple, here))
    outgoing = call(
        mid_kernel,
        jax.ShapeDtypeStruct((rows, rank, vecs), bf16),
        [vmem, vmem, vmem, vmem],
        [VMEM((cols * rank, vecs), bf16)],
        (2**29, 3000000),
        "mid",
    )(gathered, leaf_couple, first, second)
    received = lax.all_to_all(outgoing, "row", split_axis=0, concat_axis=0, tiled=True)

    near, ordered = call(
        near_kernel,
        [jax.ShapeDtypeStruct((vecs, leaf), f32), jax.ShapeDtypeStruct(coupling.shape[1:], bf16)],
        [smem, smem, smem, vmem, vmem, vmem, vmem, vmem],
        [SMEM((near_blocks.shape[2],), jnp.int32)],
        (2**36, 2 * 9 * leaf * (leaf + vecs)),
        "near",
    )(near_source, near_count, distant_region_list, near_blocks, here, row_one, row_two, coupling)

    return call(
        final_kernel,
        jax.ShapeDtypeStruct((1, 1, vecs, leaf), bf16),
        [vmem] * 5,
        [],
        (2 * 1024 * 64 * 128 + 4 * 64 * 128 * 384, 1000000),
        "final",
    )(received, ordered, transfer_row, basis_row, near)


def solution(mesh):
    placed = (
        P("row", "col", None, None),
        P("row", "col", None, None, None),
        P("row", "col", None),
        P("row", "col"),
        P("row", "col", None, None),
        P("row", "col", None, None),
        P("row", "col", None, None, None, None),
        P("row", None, None, None),
        P("row", None),
        P("row", "col", None, None),
        P("row", "col", None, None),
    )
    return jax.shard_map(
        per_device,
        mesh=mesh,
        in_specs=placed,
        out_specs=P("row", "col", None, None),
        check_vma=False,
    )
```

```python
import jax
import jax.numpy as jnp
from jax import lax
from jax.experimental import pallas as pl
from jax.experimental.pallas import tpu as pltpu
from jax.sharding import PartitionSpec as P

VMEM = pltpu.VMEM
SMEM = pltpu.SMEM
VL = 8
LINES = 8
HALF_BAND = 15


def shifted(value, axis, steps):
    count = lax.axis_size(axis)
    return lax.ppermute(value, axis, [((i + steps) % count, i) for i in range(count)])


def contract_rows(left, right):
    return lax.dot_general(left, right, (((0,), (0,)), ((), ())), preferred_element_type=jnp.float32)


def two_parts(exact, value):
    high = value.astype(jnp.bfloat16)
    low = (value - high.astype(jnp.float32)).astype(jnp.bfloat16)
    return jnp.concatenate([high, low], axis=0), jnp.concatenate([exact, exact], axis=0)


def leaf_kernel(vectors, basis, transfer, out):
    coeff = lax.dot_general(
        basis[0, 0], vectors[0, 0], (((1,), (1,)), ((), ())), preferred_element_type=jnp.float32
    ).astype(jnp.bfloat16)
    half = transfer.shape[2] // 2
    packed = jnp.concatenate([transfer[0, 0, :half], transfer[0, 0, half:]], axis=1)
    chunk = jnp.concatenate([coeff, packed], axis=0)
    for i in range(out.shape[0]):
        out[i] = chunk


def fold_kernel(gathered, out, chunk, sems):
    lines, depth = gathered.shape[0], gathered.shape[1]
    rank = 2 * depth // 3
    half = rank // 2
    size = lines * rank

    def send(part, start, length):
        return [
            pltpu.make_async_copy(
                chunk.at[pl.ds(start, length)], out.at[i, pl.ds(start, length)], sems.at[part, i]
            )
            for i in range(out.shape[0])
        ]

    chunk[:size] = gathered[:, :rank].reshape(size, -1)
    leaves = send(0, 0, size)
    for copy in leaves:
        copy.start()
    low = gathered[:, :half].reshape(lines * half, -1)
    high = gathered[:, half:rank].reshape(lines * half, -1)
    packed = gathered[:, rank:].reshape(lines * half, -1)
    region = contract_rows(packed[:, :rank], low) + contract_rows(packed[:, rank:], high)
    chunk[size:] = region.astype(chunk.dtype)
    regions = send(1, size, rank)
    for copy in regions:
        copy.start()
    for copy in leaves + regions:
        copy.wait()


def pack_kernel(couple, out_first, out_second):
    bands, rank = couple.shape[3], couple.shape[4]
    size = HALF_BAND * rank
    rest = (bands - HALF_BAND) * rank
    for d, out in ((1, out_first), (2, out_second)):
        out[:, :rank] = couple[0, 0, d, :HALF_BAND].reshape(size, rank)
        out[:rest, rank:] = couple[0, 0, d, HALF_BAND:].reshape(rest, rank)
        out[rest:, rank:] = jnp.zeros((size - rest, rank), out.dtype)


def mid_kernel(gathered, own, first, second, out, turned):
    row, col = lax.axis_index("row"), lax.axis_index("col")
    bands, rank = own.shape[3], own.shape[4]
    groups, lines = gathered.shape[0], gathered.shape[1] // rank - 1
    cols, rows = groups * lines, out.shape[0]
    for j in range(cols):
        source = lax.rem(col + 3 + j, cols)
        start = pl.multiple_of(lax.rem(source, lines) * rank, rank)
        turned[j * rank : (j + 1) * rank] = gathered[source // lines, pl.ds(start, rank)]
    region = sum(gathered[x, lines * rank :].astype(jnp.float32) for x in range(groups)).astype(out.dtype)
    for a in range(rows):
        out[a] = region
    out[row] = contract_rows(own[0, 0, 0].reshape(bands * rank, rank), turned[: bands * rank]).astype(out.dtype)
    size = HALF_BAND * rank
    both = jnp.concatenate([first[...], second[...]], axis=1)
    low = contract_rows(both, turned[:size])
    high = contract_rows(both, turned[size : 2 * size])
    for d in (1, 2):
        start = 2 * (d - 1) * rank
        term = low[start : start + rank] + high[start + rank : start + 2 * rank]
        out[lax.rem(row + rows - d, rows)] = term.astype(out.dtype)


def near_kernel(source, count, listing, blocks, here, one, two, coupling, out, ordered, slot_of):
    slots = blocks.shape[2]
    rows = coupling.shape[1]
    row = lax.axis_index("row")
    for f in range(rows):
        region = listing[0, f]
        is_far = lax.rem(region - row + rows, rows) >= 3
        ordered[region] = jnp.where(is_far, coupling[0, f], jnp.zeros_like(coupling[0, f]))
    for s in range(slots):
        slot_of[source[0, 0, s]] = s
    live_count = count[0, 0]
    out[...] = jnp.zeros_like(out)
    for cell in range(slots):
        bundle = (here, one, two)[cell // 3]
        slot = slot_of[cell]

        @pl.when(slot < live_count)
        def _():
            out[...] += jnp.dot(bundle[cell % 3], blocks[0, 0, slot], preferred_element_type=jnp.float32)


def final_kernel(received, ordered, transfer, basis, near, out):
    row = lax.axis_index("row")
    rows, rank = received.shape[0], received.shape[1]
    band = received[row].astype(jnp.float32)
    for d in (1, 2):
        band += received[lax.rem(row + d, rows)].astype(jnp.float32)
    outgoing = contract_rows(
        ordered[...].reshape(rows * rank, rank), received[...].reshape(rows * rank, received.shape[2])
    )
    parts, weights = two_parts(transfer[0, 0], outgoing)
    leaf_out = band + contract_rows(weights, parts)
    parts, weights = two_parts(basis[0, 0], leaf_out)
    far = contract_rows(parts, weights)
    out[0, 0] = (near[...] + far).astype(out.dtype)


def whole(shape):
    return pl.BlockSpec(shape, lambda i: (0,) * len(shape))


def call(kernel, out_shape, in_specs, scratch, cost, name, out_space=VMEM):
    return pl.pallas_call(
        kernel,
        out_shape=out_shape,
        in_specs=in_specs,
        out_specs=jax.tree.map(lambda _: pl.BlockSpec(memory_space=out_space), out_shape),
        scratch_shapes=scratch,
        cost_estimate=pl.CostEstimate(flops=cost[0], bytes_accessed=cost[1], transcendentals=0),
        compiler_params=pltpu.CompilerParams(vmem_limit_bytes=VL * 1024 * 1024),
        name=name,
    )


def per_device(
    vectors,
    near_blocks,
    near_source,
    near_count,
    basis_col,
    transfer_col,
    leaf_couple,
    coupling,
    distant_region_list,
    transfer_row,
    basis_row,
):
    rows, cols = lax.axis_size("row"), lax.axis_size("col")
    vecs, leaf = vectors.shape[2:]
    rank = basis_col.shape[2]
    bands = leaf_couple.shape[3]
    bf16, f32 = jnp.bfloat16, jnp.float32
    vmem, smem = pl.BlockSpec(memory_space=VMEM), pl.BlockSpec(memory_space=SMEM)

    col_one = shifted(vectors[0, 0], "col", 1)
    col_two = shifted(vectors[0, 0], "col", 2)

    chunk_shape = (LINES, rank + rank // 2, vecs)
    groups = cols // LINES
    chunks = pl.pallas_call(
        leaf_kernel,
        grid=(1,),
        out_shape=jax.ShapeDtypeStruct(chunk_shape, bf16),
        in_specs=[whole(a.shape) for a in (vectors, basis_col, transfer_col)],
        out_specs=whole(chunk_shape),
        cost_estimate=pl.CostEstimate(flops=2 * rank * vecs * leaf, bytes_accessed=1000000, transcendentals=0),
        name="leaf",
    )(vectors, basis_col, transfer_col)
    near_cols = [[x * LINES + z for z in range(LINES)] for x in range(groups)]
    far_cols = [[x * LINES + z for x in range(groups)] for z in range(LINES)]
    line = lax.all_to_all(chunks, "col", 0, 0, axis_index_groups=near_cols, tiled=True)
    folded_shape = (groups, (LINES + 1) * rank, vecs)
    folded = call(
        fold_kernel,
        jax.ShapeDtypeStruct(folded_shape, bf16),
        [vmem],
        [VMEM(folded_shape[1:], bf16), pltpu.SemaphoreType.DMA((2, groups))],
        (2 * LINES * rank * rank * vecs, 1000000),
        "fold",
        pl.ANY,
    )(line)
    gathered = lax.all_to_all(folded, "col", 0, 0, axis_index_groups=far_cols, tiled=True)

    packed_shape = jax.ShapeDtypeStruct((HALF_BAND * rank, 2 * rank), bf16)
    packed_one, packed_two = call(
        pack_kernel,
        [packed_shape] * 2,
        [vmem],
        [],
        (0, 2000000),
        "pack",
    )(leaf_couple)
    col_one, col_two, packed_one, packed_two = lax.optimization_barrier((col_one, col_two, packed_one, packed_two))
    first = shifted(packed_one, "row", -1)
    second = shifted(packed_two, "row", -2)

    here = jnp.stack([vectors[0, 0], col_one, col_two])
    row_one = shifted(here, "row", 1)
    row_two = shifted(here, "row", 2)

    leaf_couple, here = lax.optimization_barrier((leaf_couple, here))
    outgoing = call(
        mid_kernel,
        jax.ShapeDtypeStruct((rows, rank, vecs), bf16),
        [vmem, vmem, vmem, vmem],
        [VMEM((cols * rank, vecs), bf16)],
        (2**29, 3000000),
        "mid",
    )(gathered, leaf_couple, first, second)
    received = lax.all_to_all(outgoing, "row", split_axis=0, concat_axis=0, tiled=True)

    near, ordered = call(
        near_kernel,
        [jax.ShapeDtypeStruct((vecs, leaf), f32), jax.ShapeDtypeStruct(coupling.shape[1:], bf16)],
        [smem, smem, smem, vmem, vmem, vmem, vmem, vmem],
        [SMEM((near_blocks.shape[2],), jnp.int32)],
        (2**36, 2 * 9 * leaf * (leaf + vecs)),
        "near",
    )(near_source, near_count, distant_region_list, near_blocks, here, row_one, row_two, coupling)

    return call(
        final_kernel,
        jax.ShapeDtypeStruct((1, 1, vecs, leaf), bf16),
        [vmem] * 5,
        [],
        (2 * 1024 * 64 * 128 + 4 * 64 * 128 * 384, 1000000),
        "final",
    )(received, ordered, transfer_row, basis_row, near)


def solution(mesh):
    placed = (
        P("row", "col", None, None),
        P("row", "col", None, None, None),
        P("row", "col", None),
        P("row", "col"),
        P("row", "col", None, None),
        P("row", "col", None, None),
        P("row", "col", None, None, None, None),
        P("row", None, None, None),
        P("row", None),
        P("row", "col", None, None),
        P("row", "col", None, None),
    )
    return jax.shard_map(
        per_device,
        mesh=mesh,
        in_specs=placed,
        out_specs=P("row", "col", None, None),
        check_vma=False,
    )
```
